32 devices in a mesh: layer: 8 (over z, y), rep: 4 (over x, core).
Axes of the slice: x: 2, y: 2, z: 4, core: 2. Of those that a mesh axis runs over, the one named last changes fastest.
Arguments:
- features: bfloat16 [4096, 128], P('layer'), may hold values from -6 to 6
- weight: bfloat16 [128, 256], replicated, may hold values from -0.5 to 0.5
- out_bias: float32 [256], replicated, may hold values from -3 to 3
- tile_values: bfloat16 [8, 8, 2, 128, 128], P('layer', 'rep'), may hold values from -0.375 to 0.375
- tile_rows: int32 [8, 8, 2], P('layer', 'rep'), may hold values from 0 to 3
- tile_cols: int32 [8, 8, 2], P('layer', 'rep'), may hold values from 0 to 3
- tile_counts: int32 [8, 8, 2], P('layer', 'rep'), may hold values from 0 to 128
- cotangent: bfloat16 [4096, 256], P('layer'), may hold values from -18 to 18
Outputs:
- activation: bfloat16 [4096, 256], P('layer')
- grad_features: bfloat16 [4096, 128], P('layer')
- grad_weight: float32 [128, 256], replicated
- grad_bias: float32 [256], replicated
The draws below stay inside these ranges and needn't reach their ends.
All inputs are finite; a program needn't handle non-finite values.
Results may differ from the reference program's by a relative error of at most 0.0059.
Values may be sent and summed in bfloat16 or wider, within the bound.
A program may use at most 64 MiB of HBM per device.

```python
import math
import jax
import jax.numpy as jnp
from jax import lax

F_IN = 128
HID = 256
TILE = 128
NODE_DEV = 512
SLOTS = 2
NODES = 4096
N_LAYER = 8


def draw_cotangent(key, part):
    row_scale = 1.0 + 2.0 * jnp.arange(NODES, dtype=jnp.float32)[:, None] / (NODES - 1)
    normal_part = jax.random.normal(jax.random.fold_in(key, 3), (NODES, HID), jnp.float32)
    values = jnp.clip(normal_part, -5.0, 5.0) * row_scale
    return values.astype(jnp.bfloat16)


def with_ends(result, own_key, low, largest):
    place = [jax.random.randint(jax.random.fold_in(own_key, axis), (), 0, length) for axis, length in enumerate(result.shape)]
    main_axis = result.shape.index(max(result.shape))
    beside = place[:main_axis] + [(place[main_axis] + 1) % result.shape[main_axis]] + place[main_axis + 1:]
    return result.at[tuple(place)].set(low).at[tuple(beside)].set(largest)


def block_scale(key, extent, shards, smallest, top_value):
    level, own = 1.0, jax.random.fold_in(key, 6)
    for axis_at, blocks in shards:
        draws = jnp.exp(jax.random.uniform(jax.random.fold_in(own, axis_at), (blocks,), jnp.float32, smallest / len(shards), top_value / len(shards)))
        level = level * jnp.repeat(draws, extent[axis_at] // blocks).reshape([-1 if axis == axis_at else 1 for axis in range(len(extent))])
    return level


def scatter_about(own_key, shape, spread, limit, pieces=(), kind=jnp.bfloat16):
    array = jax.random.normal(own_key, shape, jnp.float32) * spread
    if len(pieces) > 0:
        array = block_scale(own_key, shape, pieces, -0.22, 0.18) * array
    return jnp.clip(array, min=-limit, max=limit).astype(kind)


def setup_inputs(seed: int = 0) -> dict:
    streams_of = jax.random.split(jax.random.key(seed), 9)
    features = scatter_about(streams_of[0], (NODES, F_IN), 1.0, 6.0, ((0, 8),))
    weight = scatter_about(streams_of[1], (F_IN, HID), F_IN ** -0.5, 0.5)
    out_bias = scatter_about(streams_of[2], (HID,), 0.5, 3.0, (), jnp.float32)
    tile_values = scatter_about(streams_of[3], (N_LAYER, N_LAYER, SLOTS, TILE, TILE), (N_LAYER * SLOTS * TILE * TILE // (2 * NODE_DEV)) ** -0.5, 0.375, ((0, 8), (1, 4)))
    tile_rows = with_ends(jax.random.randint(streams_of[4], (N_LAYER, N_LAYER, SLOTS), 0, NODE_DEV // TILE), jax.random.fold_in(streams_of[4], 1), 0, (NODE_DEV // TILE) - 1).astype(jnp.int32)
    tile_cols = with_ends(jax.random.randint(streams_of[5], (N_LAYER, N_LAYER, SLOTS), 0, NODE_DEV // TILE), jax.random.fold_in(streams_of[5], 1), 0, (NODE_DEV // TILE) - 1).astype(jnp.int32)
    tile_counts = with_ends(jax.random.randint(streams_of[6], (N_LAYER, N_LAYER, SLOTS), 0, TILE + 1), jax.random.fold_in(streams_of[6], 1), 0, TILE).astype(jnp.int32)
    cotangent = draw_cotangent(jax.random.fold_in(streams_of[8], 71), 0)
    return {"features": features, "weight": weight, "out_bias": out_bias, "tile_values": tile_values, "tile_rows": tile_rows, "tile_cols": tile_cols, "tile_counts": tile_counts, "cotangent": cotangent}


def live_tiles(tile_values, tile_counts, lane_ids):
    return jnp.where(lane_ids < tile_counts[..., None, None], tile_values, jnp.zeros((), tile_values.dtype)).astype(jnp.float32)

def reference(features, weight, out_bias, tile_values, tile_rows, tile_cols, tile_counts, cotangent):
    node_count = features.shape[0]
    row_tiles = NODE_DEV // TILE
    tile_count = node_count // TILE
    lane_ids = jnp.arange(TILE, dtype=jnp.int32)
    section_ids = jnp.arange(N_LAYER, dtype=jnp.int32)
    row_range = jnp.arange(row_tiles, dtype=jnp.int32)
    projected = jnp.dot(features, weight, preferred_element_type=jnp.float32).astype(jnp.bfloat16)
    proj_tiles = projected.reshape(tile_count, TILE, HID)

    def forward_block(block_index):
        tiles_here = live_tiles(tile_values[block_index], tile_counts[block_index], lane_ids)
        columns = (section_ids[:, None] * row_tiles + tile_cols[block_index]).astype(jnp.int32)
        picked = proj_tiles[columns].astype(jnp.float32)
        products = jnp.einsum('skij,skjf->skif', tiles_here, picked, precision=lax.Precision.HIGHEST)
        placer = (tile_rows[block_index][..., None] == row_range).astype(jnp.float32)
        return jnp.einsum('skr,skif->rif', placer, products, precision=lax.Precision.HIGHEST)
    aggregate = lax.map(forward_block, section_ids).reshape(node_count, HID)
    pre_act = projected.astype(jnp.float32) + aggregate + out_bias.astype(jnp.float32)
    sigmoid_part = jax.nn.sigmoid(pre_act)
    activation = (pre_act * sigmoid_part).astype(jnp.bfloat16)
    grad_pre = (cotangent.astype(jnp.float32) * sigmoid_part * (1.0 + pre_act * (1.0 - sigmoid_part))).astype(jnp.bfloat16)
    grad_tiles = grad_pre.reshape(tile_count, TILE, HID)

    def backward_block(running, block_index):
        tiles_here = live_tiles(tile_values[block_index], tile_counts[block_index], lane_ids)
        sources = (block_index * row_tiles + tile_rows[block_index]).astype(jnp.int32)
        picked = grad_tiles[sources].astype(jnp.float32)
        products = jnp.einsum('skij,skif->skjf', tiles_here, picked, precision=lax.Precision.HIGHEST)
        columns = (section_ids[:, None] * row_tiles + tile_cols[block_index]).astype(jnp.int32)
        running = running.at[columns.reshape(-1)].add(products.reshape(-1, TILE, HID))
        return (running, None)
    start_sum = jnp.zeros((tile_count, TILE, HID), jnp.float32)
    transposed, _ = lax.scan(backward_block, start_sum, section_ids)
    grad_projected = (grad_pre.astype(jnp.float32) + transposed.reshape(node_count, HID)).astype(jnp.bfloat16)
    grad_features = jnp.dot(grad_projected, weight.T, preferred_element_type=jnp.float32).astype(jnp.bfloat16)
    grad_scale = 1.0 / math.sqrt(node_count)
    grad_weight = jnp.dot(features.T, grad_projected, preferred_element_type=jnp.float32) * grad_scale
    grad_bias = lax.optimization_barrier(jnp.sum(grad_pre.astype(jnp.float32), axis=0)) * grad_scale
    return (activation, grad_features, grad_weight, grad_bias)
```

```python
import functools
import math

import jax
import jax.numpy as jnp
from jax import lax
from jax.experimental import pallas as pl
from jax.experimental.pallas import tpu as pltpu
from jax.sharding import PartitionSpec as P

BF = jnp.bfloat16
F32 = jnp.float32
NT = (((1,), (1,)), ((), ()))
NN = (((1,), (0,)), ((), ()))
MESH = pl.DeviceIdType.MESH


def dot(a, b, dims):
    return lax.dot_general(a, b, dims, preferred_element_type=F32)


def kernel(
    L, R, grad_scale,
    feat, w, bias, tv, rows, cols, counts, cot,
    act_o, gf_o, gw_o, gb_o,
    tiles, wt, biasb, cot_t, proj, agg, grad, act_all, gp_all, psend, precv, gwbuf, fin,
    t_send, t_fwd, t_recv, p_send, p_fwd, p_recv, q_send, q_recv,
    a_send, a_recv, g_send, g_recv, w_send, w_recv, f_send, f_recv,
):
    l = lax.axis_index("layer")
    r = lax.axis_index("rep")
    sections, slots, tile = tv.shape[1], tv.shape[2], tv.shape[3]
    hidden = w.shape[1]
    hs = hidden // R
    nt = feat.shape[0] // tile
    meta_at = slots * tile
    metas = tiles.shape[1] - meta_at
    mine = pl.ds(pl.multiple_of(r * hs, hs), hs)

    def remote(src, dst, ssem, rsem, pl_, pr_):
        return pltpu.make_async_remote_copy(
            src_ref=src, dst_ref=dst, send_sem=ssem, recv_sem=rsem,
            device_id={"layer": pl_, "rep": pr_}, device_id_type=MESH,
        )

    def each(n, fn, start=0):
        lax.fori_loop(start, n, lambda i, c: (fn(i), c)[1], 0)

    barrier = pltpu.get_barrier_semaphore()

    def greet_layer(d):
        pl.semaphore_signal(
            barrier, inc=1, device_id={"layer": lax.rem(l + d, L), "rep": r}, device_id_type=MESH)

    def greet_rep(d):
        pl.semaphore_signal(
            barrier, inc=1, device_id={"layer": l, "rep": lax.rem(r + d, R)}, device_id_type=MESH)

    each(L, greet_layer, 1)
    each(R, greet_rep, 1)

    lanes = lax.broadcasted_iota(jnp.int32, (tile, tile), 1)
    row_ids = lax.broadcasted_iota(jnp.int32, (metas, tile), 0)
    for j in range(sections):
        meta = jnp.zeros((metas, tile), F32)
        at = r * sections + j
        for k in range(slots):
            live = jnp.where(lanes < counts[0, j, k], tv[0, j, k].astype(F32), 0.0)
            tiles[at, pl.ds(k * tile, tile), :] = live.astype(BF)
            base = 2 * nt * k
            meta = meta + jnp.where(row_ids == base + rows[0, j, k], 1.0, 0.0)
            meta = meta + jnp.where(row_ids == base + nt + cols[0, j, k], 1.0, 0.0)
        tiles[at, pl.ds(meta_at, metas), :] = meta.astype(BF)

    wt[...] = jnp.transpose(w[...].astype(F32), (1, 0)).astype(BF)
    own = dot(wt[mine, :], feat[...], NT).astype(BF)
    for t in range(nt):
        proj[l, t] = own[:, t * tile:(t + 1) * tile]

    pl.semaphore_wait(barrier, L - 1 + R - 1)

    twin_l = l + 1 - 2 * lax.rem(l, 2)
    twin_r = r + 1 - 2 * lax.rem(r, 2)

    def p_direct(d):
        p = lax.rem(l + 2 * d, L)
        return remote(proj.at[l], proj.at[l], p_send.at[d], p_recv.at[l], p, r)

    def p_forward(d):
        p = lax.rem(l + 2 * d, L)
        return remote(proj.at[p], proj.at[p], p_fwd.at[d], p_recv.at[p], twin_l, r)

    def p_arrival(p):
        return remote(proj.at[p], proj.at[p], p_fwd.at[0], p_recv.at[p], twin_l, r)

    def t_block(q):
        return tiles.at[pl.ds(q * sections, sections)]

    def t_direct(d):
        return remote(t_block(r), t_block(r), t_send.at[d], t_recv.at[r], l, lax.rem(r + 2 * d, R))

    def t_forward(d):
        q = lax.rem(r + 2 * d, R)
        return remote(t_block(q), t_block(q), t_fwd.at[d], t_recv.at[q], l, twin_r)

    def t_arrival(q):
        return remote(t_block(q), t_block(q), t_fwd.at[0], t_recv.at[q], l, twin_r)

    each(R // 2, lambda d: t_direct(d).start(), 1)
    each(L // 2, lambda d: p_direct(L // 2 - d).start(), 1)
    p_forward(0).start()
    t_forward(0).start()

    biasb[...] = jnp.transpose(jnp.broadcast_to(bias[...], (tile, hidden)), (1, 0))
    for t in range(nt):
        part = cot[pl.ds(t * tile, tile), :].astype(F32)
        cot_t[t] = jnp.transpose(part, (1, 0)).astype(BF)

    def relay_tiles(d):
        t_arrival(lax.rem(r + 2 * d, R)).wait_recv()
        t_forward(d).start()

    def relay_proj(d):
        p_arrival(lax.rem(l + 2 * d, L)).wait_recv()
        p_forward(d).start()

    each(R // 2, relay_tiles, 1)
    each(L // 2, relay_proj, 1)
    each(R // 2, lambda d: t_arrival(lax.rem(twin_r + 2 * d, R)).wait_recv())

    agg[...] = jnp.zeros_like(agg)

    def section(s):
        meta = tiles[s, pl.ds(meta_at, metas), :].astype(F32)
        blocks = [proj[s, c].astype(F32) for c in range(nt)]
        sums = [agg[t] for t in range(nt)]
        for k in range(slots):
            base = 2 * nt * k
            picked = sum(
                meta[base + nt + c:base + nt + c + 1, :] * blocks[c] for c in range(nt)
            ).astype(BF)
            product = dot(picked, tiles[s, pl.ds(k * tile, tile), :], NT)
            for t in range(nt):
                sums[t] = sums[t] + meta[base + t:base + t + 1, :] * product
        for t in range(nt):
            agg[t] = sums[t]

    each(L // 2, lambda d: section(lax.rem(l + 2 * d, L)))

    def late_section(d):
        p = lax.rem(twin_l + 2 * d, L)
        p_arrival(p).wait_recv()
        section(p)

    each(L // 2, late_section)

    own_bias = biasb[mine, :]
    for t in range(nt):
        pre = proj[l, t].astype(F32) + agg[t] + own_bias
        sig = jax.nn.sigmoid(pre)
        act_all[t, mine, :] = (pre * sig).astype(BF)
        grad[t] = (cot_t[t, mine, :].astype(F32) * sig * (1.0 + pre * (1.0 - sig))).astype(BF)

    def q_copy(d):
        s = lax.rem(l + d, L)
        return remote(psend.at[s], precv.at[l], q_send.at[d], q_recv.at[l], s, r)

    def products(s, out, at):
        raw = tiles[s, pl.ds(meta_at, metas), :]
        meta = raw.astype(F32)
        blocks = [grad[t].astype(F32) for t in range(nt)]
        for k in range(slots):
            base = 2 * nt * k
            picked = sum(
                meta[base + t:base + t + 1, :] * blocks[t] for t in range(nt)
            ).astype(BF)
            out[at, pl.ds(k * hs, hs), :] = dot(
                picked, tiles[s, pl.ds(k * tile, tile), :], NN).astype(BF)
        out[at, pl.ds(slots * hs, metas), :] = raw

    def send_products(d):
        s = lax.rem(l + d, L)
        products(s, psend, s)
        q_copy(d).start()

    each(L, send_products, 1)

    def rep_copy(buf, at, ssem, rsem, d):
        return remote(buf.at[:, at, :], buf.at[:, at, :], ssem, rsem, l, lax.rem(r + d, R))

    def rep_slice(q):
        return pl.ds(pl.multiple_of(q * hs, hs), hs)

    each(R, lambda d: rep_copy(act_all, mine, a_send.at[d], a_recv.at[r], d).start(), 1)
    products(l, precv, l)

    def a_wait(d):
        q = lax.rem(r + d, R)
        rep_copy(act_all, rep_slice(q), a_send.at[d], a_recv.at[q], d).wait_recv()

    each(R, a_wait, 1)
    for t in range(nt):
        act_o[pl.ds(t * tile, tile), :] = jnp.transpose(
            act_all[t].astype(F32), (1, 0)).astype(BF)

    for t in range(nt):
        agg[t] = grad[t].astype(F32)

    def add_products(p):
        meta = precv[p, pl.ds(slots * hs, metas), :].astype(F32)
        for c in range(nt):
            total = agg[c]
            for k in range(slots):
                at = 2 * nt * k + nt + c
                total = total + meta[at:at + 1, :] * precv[p, pl.ds(k * hs, hs), :].astype(F32)
            agg[c] = total

    add_products(l)

    def take_products(d):
        p = lax.rem(l + d, L)
        remote(precv.at[p], precv.at[p], q_send.at[d], q_recv.at[p], p, r).wait_recv()
        add_products(p)

    each(L, take_products, 1)

    for t in range(nt):
        gp_all[t, mine, :] = agg[t].astype(BF)
    each(R, lambda d: rep_copy(gp_all, mine, g_send.at[d], g_recv.at[r], d).start(), 1)

    gw = jnp.zeros((hs, feat.shape[1]), F32)
    gb = jnp.zeros((metas, tile), F32)
    per = tile // hs
    ones = jnp.ones((metas, tile), BF)
    for t in range(nt):
        gw = gw + dot(gp_all[t, mine, :], feat[pl.ds(t * tile, tile), :], NN)
        gb = gb + dot(ones, jnp.concatenate([grad[t]] * per, axis=0), NT)
    half = lax.broadcasted_iota(jnp.int32, (metas, tile), 1) // hs
    gb = jnp.where(half == lax.rem(r, per), gb, 0.0)
    gwbuf[l, pl.ds(0, hs), :] = gw.astype(BF)
    gwbuf[l, pl.ds(hs, metas), :] = gb.astype(BF)

    def w_copy(d):
        return remote(gwbuf.at[l], gwbuf.at[l], w_send.at[d], w_recv.at[l], lax.rem(l + d, L), r)

    each(L, lambda d: w_copy(d).start(), 1)

    def g_wait(d):
        q = lax.rem(r + d, R)
        rep_copy(gp_all, rep_slice(q), g_send.at[d], g_recv.at[q], d).wait_recv()

    def w_wait(d):
        p = lax.rem(l + d, L)
        remote(gwbuf.at[p], gwbuf.at[p], w_send.at[d], w_recv.at[p], p, r).wait_recv()

    each(L, w_wait, 1)
    fin[r] = (
        lax.fori_loop(0, L, lambda p, c: c + gwbuf[p].astype(F32),
                      jnp.zeros((hs + metas, tile), F32)) * grad_scale
    ).astype(BF)

    def f_copy(q, d):
        return remote(fin.at[q], fin.at[q], f_send.at[d], f_recv.at[q], l, lax.rem(r + d, R))

    each(R, lambda d: f_copy(r, d).start(), 1)

    each(R, g_wait, 1)
    for t in range(nt):
        turned = jnp.transpose(gp_all[t].astype(F32), (1, 0)).astype(BF)
        gf_o[pl.ds(t * tile, tile), :] = dot(turned, w[...], NT).astype(BF)

    each(R, lambda d: f_copy(lax.rem(r + d, R), d).wait_recv(), 1)
    for m in range(R // per):
        group = [fin[per * m + i].astype(F32) for i in range(per)]
        block = jnp.concatenate([g[:hs] for g in group], axis=0)
        gw_o[:, pl.ds(m * tile, tile)] = jnp.transpose(block, (1, 0))
        gb_o[:, pl.ds(m * tile, tile)] = sum(g[hs:hs + 1] for g in group)

    each(R // 2, lambda d: t_direct(d).wait_send(), 1)
    each(R // 2, lambda d: t_forward(d).wait_send())
    each(L // 2, lambda d: p_direct(L // 2 - d).wait_send(), 1)
    each(L // 2, lambda d: p_forward(d).wait_send())
    each(L, lambda d: q_copy(d).wait_send(), 1)
    each(L, lambda d: w_copy(d).wait_send(), 1)

    def rep_sent(d):
        rep_copy(act_all, mine, a_send.at[d], a_recv.at[r], d).wait_send()
        rep_copy(gp_all, mine, g_send.at[d], g_recv.at[r], d).wait_send()
        f_copy(r, d).wait_send()

    each(R, rep_sent, 1)


def local(features, weight, out_bias, tile_values, tile_rows, tile_cols, tile_counts, cotangent):
    L, R = lax.axis_size("layer"), lax.axis_size("rep")
    rows_dev, hidden = cotangent.shape
    f_in = features.shape[1]
    tile = tile_values.shape[-1]
    slots = tile_values.shape[2]
    nt = rows_dev // tile
    hs = hidden // R
    metas = slots * 2 * nt
    vmem = pl.BlockSpec(memory_space=pltpu.VMEM)
    smem = pl.BlockSpec(memory_space=pltpu.SMEM)
    sem = pltpu.SemaphoreType.DMA
    grad_scale = 1.0 / math.sqrt(rows_dev * L)
    act, gf, gw, gb = pl.pallas_call(
        functools.partial(kernel, L, R, grad_scale),
        out_shape=(
            jax.ShapeDtypeStruct((rows_dev, hidden), BF),
            jax.ShapeDtypeStruct((rows_dev, f_in), BF),
            jax.ShapeDtypeStruct((f_in, hidden), F32),
            jax.ShapeDtypeStruct((1, hidden), F32),
        ),
        in_specs=[vmem, vmem, vmem, vmem, smem, smem, smem, vmem],
        out_specs=(vmem, vmem, vmem, vmem),
        scratch_shapes=[
            pltpu.VMEM((L, slots * tile + metas, tile), BF),
            pltpu.VMEM((hidden, f_in), BF),
            pltpu.VMEM((hidden, tile), F32),
            pltpu.VMEM((nt, hidden, tile), BF),
            pltpu.VMEM((L, nt, hs, tile), BF),
            pltpu.VMEM((nt, hs, tile), F32),
            pltpu.VMEM((nt, hs, tile), BF),
            pltpu.VMEM((nt, hidden, tile), BF),
            pltpu.VMEM((nt, hidden, tile), BF),
            pltpu.VMEM((L, slots * hs + metas, tile), BF),
            pltpu.VMEM((L, slots * hs + metas, tile), BF),
            pltpu.VMEM((L, hs + metas, tile), BF),
            pltpu.VMEM((R, hs + metas, tile), BF),
            sem((R,)), sem((R,)), sem((R,)),
            sem((L,)), sem((L,)), sem((L,)),
            sem((L,)), sem((L,)),
            sem((R,)), sem((R,)),
            sem((R,)), sem((R,)),
            sem((L,)), sem((L,)),
            sem((R,)), sem((R,)),
        ],
        compiler_params=pltpu.CompilerParams(
            collective_id=0, has_side_effects=True, vmem_limit_bytes=32 * 1024 * 1024
        ),
        name="graph_layer",
    )(features, weight, out_bias.reshape(1, hidden), tile_values, tile_rows, tile_cols,
      tile_counts, cotangent)
    return act, gf, gw, gb.reshape(hidden)


def solution(mesh):
    in_specs = (
        P("layer", None),
        P(),
        P(),
        P("layer", "rep", None, None, None),
        P("layer", "rep", None),
        P("layer", "rep", None),
        P("layer", "rep", None),
        P("layer", None),
    )
    out_specs = (P("layer", None), P("layer", None), P(), P())
    return jax.shard_map(local, mesh=mesh, in_specs=in_specs, out_specs=out_specs, check_vma=False)
```

```python
import functools
import math

import jax
import jax.numpy as jnp
from jax import lax
from jax.experimental import pallas as pl
from jax.experimental.pallas import tpu as pltpu
from jax.sharding import PartitionSpec as P

BF = jnp.bfloat16
F32 = jnp.float32
NT = (((1,), (1,)), ((), ()))
NN = (((1,), (0,)), ((), ()))
MESH = pl.DeviceIdType.MESH


def dot(a, b, dims):
    return lax.dot_general(a, b, dims, preferred_element_type=F32)


def kernel(
    L, R, grad_scale,
    feat_h, w_h, bias_h, tv_h, rows_h, cols_h, counts_h, cot_h,
    act_o, gf_o, gw_o, gb_o,
    feat, w, bias, tv, rows, cols, counts, cot, in_sem,
    tiles, wt, biasb, cot_t, proj, agg, grad, act_all, gp_all, psend, precv, gwbuf, fin,
    t_send, t_fwd, t_recv, p_send, p_fwd, p_recv, q_send, q_recv,
    a_send, a_recv, g_send, g_recv, w_send, w_recv, f_send, f_recv,
):
    l = lax.axis_index("layer")
    r = lax.axis_index("rep")
    sections, slots, tile = tv.shape[1], tv.shape[2], tv.shape[3]
    hidden = w.shape[1]
    hs = hidden // R
    nt = feat.shape[0] // tile
    meta_at = slots * tile
    metas = tiles.shape[1] - meta_at
    mine = pl.ds(pl.multiple_of(r * hs, hs), hs)

    def remote(src, dst, ssem, rsem, pl_, pr_):
        return pltpu.make_async_remote_copy(
            src_ref=src, dst_ref=dst, send_sem=ssem, recv_sem=rsem,
            device_id={"layer": pl_, "rep": pr_}, device_id_type=MESH,
        )

    def each(n, fn, start=0):
        lax.fori_loop(start, n, lambda i, c: (fn(i), c)[1], 0)

    barrier = pltpu.get_barrier_semaphore()
    loads = [
        pltpu.make_async_copy(src, dst, in_sem.at[i])
        for i, (src, dst) in enumerate((
            (counts_h, counts), (rows_h, rows), (cols_h, cols), (tv_h, tv),
            (w_h, w), (feat_h, feat), (bias_h, bias), (cot_h, cot)))
    ]
    for load in loads:
        load.start()

    def greet_layer(d):
        pl.semaphore_signal(
            barrier, inc=1, device_id={"layer": lax.rem(l + d, L), "rep": r}, device_id_type=MESH)

    def greet_rep(d):
        pl.semaphore_signal(
            barrier, inc=1, device_id={"layer": l, "rep": lax.rem(r + d, R)}, device_id_type=MESH)

    each(L, greet_layer, 1)
    each(R, greet_rep, 1)

    for load in loads[:4]:
        load.wait()
    lanes = lax.broadcasted_iota(jnp.int32, (tile, tile), 1)
    row_ids = lax.broadcasted_iota(jnp.int32, (metas, tile), 0)
    for j in range(sections):
        meta = jnp.zeros((metas, tile), F32)
        at = r * sections + j
        for k in range(slots):
            live = jnp.where(lanes < counts[0, j, k], tv[0, j, k].astype(F32), 0.0)
            tiles[at, pl.ds(k * tile, tile), :] = live.astype(BF)
            base = 2 * nt * k
            meta = meta + jnp.where(row_ids == base + rows[0, j, k], 1.0, 0.0)
            meta = meta + jnp.where(row_ids == base + nt + cols[0, j, k], 1.0, 0.0)
        tiles[at, pl.ds(meta_at, metas), :] = meta.astype(BF)

    for load in loads[4:6]:
        load.wait()
    wt[...] = jnp.transpose(w[...].astype(F32), (1, 0)).astype(BF)
    own = dot(wt[mine, :], feat[...], NT).astype(BF)
    for t in range(nt):
        proj[l, t] = own[:, t * tile:(t + 1) * tile]

    pl.semaphore_wait(barrier, L - 1 + R - 1)

    twin_l = l + 1 - 2 * lax.rem(l, 2)
    twin_r = r + 1 - 2 * lax.rem(r, 2)

    def p_direct(d):
        p = lax.rem(l + 2 * d, L)
        return remote(proj.at[l], proj.at[l], p_send.at[d], p_recv.at[l], p, r)

    def p_forward(d):
        p = lax.rem(l + 2 * d, L)
        return remote(proj.at[p], proj.at[p], p_fwd.at[d], p_recv.at[p], twin_l, r)

    def p_arrival(p):
        return remote(proj.at[p], proj.at[p], p_fwd.at[0], p_recv.at[p], twin_l, r)

    def t_block(q):
        return tiles.at[pl.ds(q * sections, sections)]

    def t_direct(d):
        return remote(t_block(r), t_block(r), t_send.at[d], t_recv.at[r], l, lax.rem(r + 2 * d, R))

    def t_forward(d):
        q = lax.rem(r + 2 * d, R)
        return remote(t_block(q), t_block(q), t_fwd.at[d], t_recv.at[q], l, twin_r)

    def t_arrival(q):
        return remote(t_block(q), t_block(q), t_fwd.at[0], t_recv.at[q], l, twin_r)

    each(R // 2, lambda d: t_direct(d).start(), 1)
    each(L // 2, lambda d: p_direct(L // 2 - d).start(), 1)
    p_forward(0).start()
    t_forward(0).start()

    for load in loads[6:]:
        load.wait()
    biasb[...] = jnp.transpose(jnp.broadcast_to(bias[...], (tile, hidden)), (1, 0))
    for t in range(nt):
        part = cot[pl.ds(t * tile, tile), :].astype(F32)
        cot_t[t] = jnp.transpose(part, (1, 0)).astype(BF)

    def relay_tiles(d):
        t_arrival(lax.rem(r + 2 * d, R)).wait_recv()
        t_forward(d).start()

    def relay_proj(d):
        p_arrival(lax.rem(l + 2 * d, L)).wait_recv()
        p_forward(d).start()

    each(R // 2, relay_tiles, 1)
    each(L // 2, relay_proj, 1)
    each(R // 2, lambda d: t_arrival(lax.rem(twin_r + 2 * d, R)).wait_recv())

    agg[...] = jnp.zeros_like(agg)

    def section(s):
        meta = tiles[s, pl.ds(meta_at, metas), :].astype(F32)
        blocks = [proj[s, c].astype(F32) for c in range(nt)]
        sums = [agg[t] for t in range(nt)]
        for k in range(slots):
            base = 2 * nt * k
            picked = sum(
                meta[base + nt + c:base + nt + c + 1, :] * blocks[c] for c in range(nt)
            ).astype(BF)
            product = dot(picked, tiles[s, pl.ds(k * tile, tile), :], NT)
            for t in range(nt):
                sums[t] = sums[t] + meta[base + t:base + t + 1, :] * product
        for t in range(nt):
            agg[t] = sums[t]

    each(L // 2, lambda d: section(lax.rem(l + 2 * d, L)))

    def late_section(d):
        p = lax.rem(twin_l + 2 * d, L)
        p_arrival(p).wait_recv()
        section(p)

    each(L // 2, late_section)

    own_bias = biasb[mine, :]
    for t in range(nt):
        pre = proj[l, t].astype(F32) + agg[t] + own_bias
        sig = jax.nn.sigmoid(pre)
        act_all[t, mine, :] = (pre * sig).astype(BF)
        grad[t] = (cot_t[t, mine, :].astype(F32) * sig * (1.0 + pre * (1.0 - sig))).astype(BF)

    def q_copy(d):
        s = lax.rem(l + d, L)
        return remote(psend.at[s], precv.at[l], q_send.at[d], q_recv.at[l], s, r)

    def products(s, out, at):
        raw = tiles[s, pl.ds(meta_at, metas), :]
        meta = raw.astype(F32)
        blocks = [grad[t].astype(F32) for t in range(nt)]
        for k in range(slots):
            base = 2 * nt * k
            picked = sum(
                meta[base + t:base + t + 1, :] * blocks[t] for t in range(nt)
            ).astype(BF)
            out[at, pl.ds(k * hs, hs), :] = dot(
                picked, tiles[s, pl.ds(k * tile, tile), :], NN).astype(BF)
        out[at, pl.ds(slots * hs, metas), :] = raw

    def send_products(d):
        s = lax.rem(l + d, L)
        products(s, psend, s)
        q_copy(d).start()

    each(L, send_products, 1)

    def rep_copy(buf, at, ssem, rsem, d):
        return remote(buf.at[:, at, :], buf.at[:, at, :], ssem, rsem, l, lax.rem(r + d, R))

    def rep_slice(q):
        return pl.ds(pl.multiple_of(q * hs, hs), hs)

    each(R, lambda d: rep_copy(act_all, mine, a_send.at[d], a_recv.at[r], d).start(), 1)
    products(l, precv, l)

    def a_wait(d):
        q = lax.rem(r + d, R)
        rep_copy(act_all, rep_slice(q), a_send.at[d], a_recv.at[q], d).wait_recv()

    each(R, a_wait, 1)
    for t in range(nt):
        act_o[pl.ds(t * tile, tile), :] = jnp.transpose(
            act_all[t].astype(F32), (1, 0)).astype(BF)

    for t in range(nt):
        agg[t] = grad[t].astype(F32)

    def add_products(p):
        meta = precv[p, pl.ds(slots * hs, metas), :].astype(F32)
        for c in range(nt):
            total = agg[c]
            for k in range(slots):
                at = 2 * nt * k + nt + c
                total = total + meta[at:at + 1, :] * precv[p, pl.ds(k * hs, hs), :].astype(F32)
            agg[c] = total

    add_products(l)

    def take_products(d):
        p = lax.rem(l + d, L)
        remote(precv.at[p], precv.at[p], q_send.at[d], q_recv.at[p], p, r).wait_recv()
        add_products(p)

    each(L, take_products, 1)

    for t in range(nt):
        gp_all[t, mine, :] = agg[t].astype(BF)
    each(R, lambda d: rep_copy(gp_all, mine, g_send.at[d], g_recv.at[r], d).start(), 1)

    gw = jnp.zeros((hs, feat.shape[1]), F32)
    gb = jnp.zeros((metas, tile), F32)
    per = tile // hs
    ones = jnp.ones((metas, tile), BF)
    for t in range(nt):
        gw = gw + dot(gp_all[t, mine, :], feat[pl.ds(t * tile, tile), :], NN)
        gb = gb + dot(ones, jnp.concatenate([grad[t]] * per, axis=0), NT)
    half = lax.broadcasted_iota(jnp.int32, (metas, tile), 1) // hs
    gb = jnp.where(half == lax.rem(r, per), gb, 0.0)
    gwbuf[l, pl.ds(0, hs), :] = gw.astype(BF)
    gwbuf[l, pl.ds(hs, metas), :] = gb.astype(BF)

    def w_copy(d):
        return remote(gwbuf.at[l], gwbuf.at[l], w_send.at[d], w_recv.at[l], lax.rem(l + d, L), r)

    each(L, lambda d: w_copy(d).start(), 1)

    def g_wait(d):
        q = lax.rem(r + d, R)
        rep_copy(gp_all, rep_slice(q), g_send.at[d], g_recv.at[q], d).wait_recv()

    def w_wait(d):
        p = lax.rem(l + d, L)
        remote(gwbuf.at[p], gwbuf.at[p], w_send.at[d], w_recv.at[p], p, r).wait_recv()

    each(L, w_wait, 1)
    fin[r] = (
        lax.fori_loop(0, L, lambda p, c: c + gwbuf[p].astype(F32),
                      jnp.zeros((hs + metas, tile), F32)) * grad_scale
    ).astype(BF)

    def f_copy(q, d):
        return remote(fin.at[q], fin.at[q], f_send.at[d], f_recv.at[q], l, lax.rem(r + d, R))

    each(R, lambda d: f_copy(r, d).start(), 1)

    each(R, g_wait, 1)
    for t in range(nt):
        turned = jnp.transpose(gp_all[t].astype(F32), (1, 0)).astype(BF)
        gf_o[pl.ds(t * tile, tile), :] = dot(turned, w[...], NT).astype(BF)

    each(R, lambda d: f_copy(lax.rem(r + d, R), d).wait_recv(), 1)
    for m in range(R // per):
        group = [fin[per * m + i].astype(F32) for i in range(per)]
        block = jnp.concatenate([g[:hs] for g in group], axis=0)
        gw_o[:, pl.ds(m * tile, tile)] = jnp.transpose(block, (1, 0))
        gb_o[:, pl.ds(m * tile, tile)] = sum(g[hs:hs + 1] for g in group)

    each(R // 2, lambda d: t_direct(d).wait_send(), 1)
    each(R // 2, lambda d: t_forward(d).wait_send())
    each(L // 2, lambda d: p_direct(L // 2 - d).wait_send(), 1)
    each(L // 2, lambda d: p_forward(d).wait_send())
    each(L, lambda d: q_copy(d).wait_send(), 1)
    each(L, lambda d: w_copy(d).wait_send(), 1)

    def rep_sent(d):
        rep_copy(act_all, mine, a_send.at[d], a_recv.at[r], d).wait_send()
        rep_copy(gp_all, mine, g_send.at[d], g_recv.at[r], d).wait_send()
        f_copy(r, d).wait_send()

    each(R, rep_sent, 1)


def write_kernel(*refs):
    n = (len(refs) - 1) // 2
    copies = [pltpu.make_async_copy(refs[i], refs[n + i], refs[-1].at[i]) for i in range(n)]
    for copy in copies:
        copy.start()
    for copy in copies:
        copy.wait()


def write_out(*arrays):
    n = len(arrays)
    return pl.pallas_call(
        write_kernel,
        out_shape=tuple(jax.ShapeDtypeStruct(a.shape, a.dtype) for a in arrays),
        in_specs=[pl.BlockSpec(memory_space=pltpu.VMEM)] * n,
        out_specs=(pl.BlockSpec(memory_space=pltpu.HBM),) * n,
        scratch_shapes=[pltpu.SemaphoreType.DMA((n,))],
        name="write_out",
    )(*[pltpu.with_memory_space_constraint(a, pltpu.VMEM) for a in arrays])


def local(features, weight, out_bias, tile_values, tile_rows, tile_cols, tile_counts, cotangent):
    L, R = lax.axis_size("layer"), lax.axis_size("rep")
    rows_dev, hidden = cotangent.shape
    f_in = features.shape[1]
    tile = tile_values.shape[-1]
    slots = tile_values.shape[2]
    nt = rows_dev // tile
    hs = hidden // R
    metas = slots * 2 * nt
    vmem = pl.BlockSpec(memory_space=pltpu.VMEM)
    hbm = pl.BlockSpec(memory_space=pltpu.HBM)
    sem = pltpu.SemaphoreType.DMA
    grad_scale = 1.0 / math.sqrt(rows_dev * L)
    act, gf, gw, gb = pl.pallas_call(
        functools.partial(kernel, L, R, grad_scale),
        out_shape=(
            jax.ShapeDtypeStruct((rows_dev, hidden), BF),
            jax.ShapeDtypeStruct((rows_dev, f_in), BF),
            jax.ShapeDtypeStruct((f_in, hidden), F32),
            jax.ShapeDtypeStruct((1, hidden), F32),
        ),
        in_specs=[hbm] * 8,
        out_specs=(vmem, vmem, vmem, vmem),
        scratch_shapes=[
            pltpu.VMEM(features.shape, BF),
            pltpu.VMEM(weight.shape, BF),
            pltpu.VMEM((1, hidden), F32),
            pltpu.VMEM(tile_values.shape, BF),
            pltpu.SMEM(tile_rows.shape, jnp.int32),
            pltpu.SMEM(tile_rows.shape, jnp.int32),
            pltpu.SMEM(tile_rows.shape, jnp.int32),
            pltpu.VMEM(cotangent.shape, BF),
            sem((8,)),
            pltpu.VMEM((L, slots * tile + metas, tile), BF),
            pltpu.VMEM((hidden, f_in), BF),
            pltpu.VMEM((hidden, tile), F32),
            pltpu.VMEM((nt, hidden, tile), BF),
            pltpu.VMEM((L, nt, hs, tile), BF),
            pltpu.VMEM((nt, hs, tile), F32),
            pltpu.VMEM((nt, hs, tile), BF),
            pltpu.VMEM((nt, hidden, tile), BF),
            pltpu.VMEM((nt, hidden, tile), BF),
            pltpu.VMEM((L, slots * hs + metas, tile), BF),
            pltpu.VMEM((L, slots * hs + metas, tile), BF),
            pltpu.VMEM((L, hs + metas, tile), BF),
            pltpu.VMEM((R, hs + metas, tile), BF),
            sem((R,)), sem((R,)), sem((R,)),
            sem((L,)), sem((L,)), sem((L,)),
            sem((L,)), sem((L,)),
            sem((R,)), sem((R,)),
            sem((R,)), sem((R,)),
            sem((L,)), sem((L,)),
            sem((R,)), sem((R,)),
        ],
        compiler_params=pltpu.CompilerParams(
            collective_id=0, has_side_effects=True, vmem_limit_bytes=32 * 1024 * 1024
        ),
        name="graph_layer",
    )(*[pltpu.with_memory_space_constraint(x, pltpu.HBM) for x in (
        features, weight, out_bias.reshape(1, hidden), tile_values, tile_rows, tile_cols,
        tile_counts, cotangent)])
    return write_out(act, gf, gw, gb.reshape(hidden))


def solution(mesh):
    in_specs = (
        P("layer", None),
        P(),
        P(),
        P("layer", "rep", None, None, None),
        P("layer", "rep", None),
        P("layer", "rep", None),
        P("layer", "rep", None),
        P("layer", None),
    )
    out_specs = (P("layer", None), P("layer", None), P(), P())
    return jax.shard_map(local, mesh=mesh, in_specs=in_specs, out_specs=out_specs, check_vma=False)
```

```python
import functools
import math

import jax
import jax.numpy as jnp
from jax import lax
from jax.experimental import pallas as pl
from jax.experimental.pallas import tpu as pltpu
from jax.sharding import PartitionSpec as P

BF = jnp.bfloat16
F32 = jnp.float32
NT = (((1,), (1,)), ((), ()))
NN = (((1,), (0,)), ((), ()))
MESH = pl.DeviceIdType.MESH


def dot(a, b, dims):
    return lax.dot_general(a, b, dims, preferred_element_type=F32)


def kernel(
    L, R, grad_scale,
    feat_h, w_h, bias_h, tv_h, rows_h, cols_h, counts_h, cot_h,
    act_o, gf_o, gw_o, gb_o,
    feat, w, bias, tv, rows, cols, counts, cot, in_sem,
    tiles, wt, biasb, cot_t, proj, agg, grad, act_all, gp_all, psend, precv, gwbuf, fin,
    t_send, t_fwd, t_recv, p_send, p_fwd, p_recv, q_send, q_recv,
    a_send, a_recv, g_send, g_recv, w_send, w_recv, f_send, f_recv,
):
    l = lax.axis_index("layer")
    r = lax.axis_index("rep")
    sections, slots, tile = tv.shape[1], tv.shape[2], tv.shape[3]
    hidden = w.shape[1]
    hs = hidden // R
    nt = feat.shape[0] // tile
    meta_at = slots * tile
    metas = tiles.shape[1] - meta_at
    mine = pl.ds(pl.multiple_of(r * hs, hs), hs)

    def remote(src, dst, ssem, rsem, pl_, pr_):
        return pltpu.make_async_remote_copy(
            src_ref=src, dst_ref=dst, send_sem=ssem, recv_sem=rsem,
            device_id={"layer": pl_, "rep": pr_}, device_id_type=MESH,
        )

    def each(n, fn, start=0):
        lax.fori_loop(start, n, lambda i, c: (fn(i), c)[1], 0)

    barrier = pltpu.get_barrier_semaphore()
    loads = [
        pltpu.make_async_copy(src, dst, in_sem.at[i])
        for i, (src, dst) in enumerate((
            (counts_h, counts), (rows_h, rows), (cols_h, cols), (tv_h, tv),
            (w_h, w), (feat_h, feat), (bias_h, bias), (cot_h, cot)))
    ]
    for load in loads:
        load.start()

    def greet_layer(d):
        pl.semaphore_signal(
            barrier, inc=1, device_id={"layer": lax.rem(l + d, L), "rep": r}, device_id_type=MESH)

    def greet_rep(d):
        pl.semaphore_signal(
            barrier, inc=1, device_id={"layer": l, "rep": lax.rem(r + d, R)}, device_id_type=MESH)

    each(L, greet_layer, 1)
    each(R, greet_rep, 1)

    for load in loads[:4]:
        load.wait()
    lanes = lax.broadcasted_iota(jnp.int32, (tile, tile), 1)
    row_ids = lax.broadcasted_iota(jnp.int32, (metas, tile), 0)
    for j in range(sections):
        meta = jnp.zeros((metas, tile), F32)
        at = r * sections + j
        for k in range(slots):
            live = jnp.where(lanes < counts[0, j, k], tv[0, j, k].astype(F32), 0.0)
            tiles[at, pl.ds(k * tile, tile), :] = live.astype(BF)
            base = 2 * nt * k
            meta = meta + jnp.where(row_ids == base + rows[0, j, k], 1.0, 0.0)
            meta = meta + jnp.where(row_ids == base + nt + cols[0, j, k], 1.0, 0.0)
        tiles[at, pl.ds(meta_at, metas), :] = meta.astype(BF)

    for load in loads[4:6]:
        load.wait()
    wt[...] = jnp.transpose(w[...].astype(F32), (1, 0)).astype(BF)
    own = dot(wt[mine, :], feat[...], NT).astype(BF)
    for t in range(nt):
        proj[l, t] = own[:, t * tile:(t + 1) * tile]

    pl.semaphore_wait(barrier, L - 1 + R - 1)

    twin_l = l + 1 - 2 * lax.rem(l, 2)
    twin_r = r + 1 - 2 * lax.rem(r, 2)

    def p_direct(d):
        p = lax.rem(l + 2 * d, L)
        return remote(proj.at[l], proj.at[l], p_send.at[d], p_recv.at[l], p, r)

    def p_forward(d):
        p = lax.rem(l + 2 * d, L)
        return remote(proj.at[p], proj.at[p], p_fwd.at[d], p_recv.at[p], twin_l, r)

    def p_arrival(p):
        return remote(proj.at[p], proj.at[p], p_fwd.at[0], p_recv.at[p], twin_l, r)

    def t_block(q):
        return tiles.at[pl.ds(q * sections, sections)]

    def t_direct(d):
        return remote(t_block(r), t_block(r), t_send.at[d], t_recv.at[r], l, lax.rem(r + 2 * d, R))

    def t_forward(d):
        q = lax.rem(r + 2 * d, R)
        return remote(t_block(q), t_block(q), t_fwd.at[d], t_recv.at[q], l, twin_r)

    def t_arrival(q):
        return remote(t_block(q), t_block(q), t_fwd.at[0], t_recv.at[q], l, twin_r)

    each(R // 2, lambda d: t_direct(d).start(), 1)
    each(L // 2, lambda d: p_direct(L // 2 - d).start(), 1)
    p_forward(0).start()
    t_forward(0).start()

    for load in loads[6:]:
        load.wait()
    biasb[...] = jnp.transpose(jnp.broadcast_to(bias[...], (tile, hidden)), (1, 0))
    for t in range(nt):
        part = cot[pl.ds(t * tile, tile), :].astype(F32)
        cot_t[t] = jnp.transpose(part, (1, 0)).astype(BF)

    def relay_tiles(d):
        t_arrival(lax.rem(r + 2 * d, R)).wait_recv()
        t_forward(d).start()

    def relay_proj(d):
        p_arrival(lax.rem(l + 2 * d, L)).wait_recv()
        p_forward(d).start()

    each(R // 2, relay_tiles, 1)
    each(L // 2, relay_proj, 1)
    each(R // 2, lambda d: t_arrival(lax.rem(twin_r + 2 * d, R)).wait_recv())

    agg[...] = jnp.zeros_like(agg)

    def section(s):
        meta = tiles[s, pl.ds(meta_at, metas), :].astype(F32)
        blocks = [proj[s, c].astype(F32) for c in range(nt)]
        sums = [agg[t] for t in range(nt)]
        for k in range(slots):
            base = 2 * nt * k
            picked = sum(
                meta[base + nt + c:base + nt + c + 1, :] * blocks[c] for c in range(nt)
            ).astype(BF)
            product = dot(picked, tiles[s, pl.ds(k * tile, tile), :], NT)
            for t in range(nt):
                sums[t] = sums[t] + meta[base + t:base + t + 1, :] * product
        for t in range(nt):
            agg[t] = sums[t]

    each(L // 2, lambda d: section(lax.rem(l + 2 * d, L)))

    def late_section(d):
        p = lax.rem(twin_l + 2 * d, L)
        p_arrival(p).wait_recv()
        section(p)

    each(L // 2, late_section)

    own_bias = biasb[mine, :]
    for t in range(nt):
        pre = proj[l, t].astype(F32) + agg[t] + own_bias
        sig = jax.nn.sigmoid(pre)
        act_all[t, mine, :] = (pre * sig).astype(BF)
        grad[t] = (cot_t[t, mine, :].astype(F32) * sig * (1.0 + pre * (1.0 - sig))).astype(BF)

    def q_copy(d):
        s = lax.rem(l + d, L)
        return remote(psend.at[s], precv.at[l], q_send.at[d], q_recv.at[l], s, r)

    def products(s, out, at):
        raw = tiles[s, pl.ds(meta_at, metas), :]
        meta = raw.astype(F32)
        blocks = [grad[t].astype(F32) for t in range(nt)]
        for k in range(slots):
            base = 2 * nt * k
            picked = sum(
                meta[base + t:base + t + 1, :] * blocks[t] for t in range(nt)
            ).astype(BF)
            out[at, pl.ds(k * hs, hs), :] = dot(
                picked, tiles[s, pl.ds(k * tile, tile), :], NN).astype(BF)
        out[at, pl.ds(slots * hs, metas), :] = raw

    def send_products(d):
        s = lax.rem(l + d, L)
        products(s, psend, s)
        q_copy(d).start()

    each(L, lambda d: send_products(L - d), 1)

    def rep_copy(buf, at, ssem, rsem, d):
        return remote(buf.at[:, at, :], buf.at[:, at, :], ssem, rsem, l, lax.rem(r + d, R))

    def rep_slice(q):
        return pl.ds(pl.multiple_of(q * hs, hs), hs)

    each(R, lambda d: rep_copy(act_all, mine, a_send.at[d], a_recv.at[r], d).start(), 1)
    products(l, precv, l)

    def a_wait(d):
        q = lax.rem(r + d, R)
        rep_copy(act_all, rep_slice(q), a_send.at[d], a_recv.at[q], d).wait_recv()

    each(R, a_wait, 1)
    for t in range(nt):
        act_o[pl.ds(t * tile, tile), :] = jnp.transpose(
            act_all[t].astype(F32), (1, 0)).astype(BF)

    for t in range(nt):
        agg[t] = grad[t].astype(F32)

    def add_products(p):
        meta = precv[p, pl.ds(slots * hs, metas), :].astype(F32)
        for c in range(nt):
            total = agg[c]
            for k in range(slots):
                at = 2 * nt * k + nt + c
                total = total + meta[at:at + 1, :] * precv[p, pl.ds(k * hs, hs), :].astype(F32)
            agg[c] = total

    gb = jnp.zeros((metas, tile), F32)
    per = tile // hs
    ones = jnp.ones((metas, tile), BF)
    for t in range(nt):
        gb = gb + dot(ones, jnp.concatenate([grad[t]] * per, axis=0), NT)
    half = lax.broadcasted_iota(jnp.int32, (metas, tile), 1) // hs
    gwbuf[l, pl.ds(hs, metas), :] = jnp.where(half == lax.rem(r, per), gb, 0.0).astype(BF)

    add_products(l)

    def take_products(d):
        p = lax.rem(l + d, L)
        remote(precv.at[p], precv.at[p], q_send.at[d], q_recv.at[p], p, r).wait_recv()
        add_products(p)

    each(L, take_products, 1)

    for t in range(nt):
        gp_all[t, mine, :] = agg[t].astype(BF)
    each(R, lambda d: rep_copy(gp_all, mine, g_send.at[d], g_recv.at[r], d).start(), 1)

    gw = dot(jnp.concatenate([agg[t].astype(BF) for t in range(nt)], axis=1), feat[...], NN)
    gwbuf[l, pl.ds(0, hs), :] = gw.astype(BF)

    def w_copy(d):
        return remote(gwbuf.at[l], gwbuf.at[l], w_send.at[d], w_recv.at[l], lax.rem(l + d, L), r)

    each(L, lambda d: w_copy(d).start(), 1)

    def g_wait(d):
        q = lax.rem(r + d, R)
        rep_copy(gp_all, rep_slice(q), g_send.at[d], g_recv.at[q], d).wait_recv()

    def w_wait(d):
        p = lax.rem(l + d, L)
        remote(gwbuf.at[p], gwbuf.at[p], w_send.at[d], w_recv.at[p], p, r).wait_recv()

    each(L, w_wait, 1)
    fin[r] = (
        lax.fori_loop(0, L, lambda p, c: c + gwbuf[p].astype(F32),
                      jnp.zeros((hs + metas, tile), F32)) * grad_scale
    ).astype(BF)

    def f_copy(q, d):
        return remote(fin.at[q], fin.at[q], f_send.at[d], f_recv.at[q], l, lax.rem(r + d, R))

    each(R, lambda d: f_copy(r, d).start(), 1)

    each(R, g_wait, 1)
    for t in range(nt):
        turned = jnp.transpose(gp_all[t].astype(F32), (1, 0)).astype(BF)
        gf_o[pl.ds(t * tile, tile), :] = dot(turned, w[...], NT).astype(BF)

    each(R, lambda d: f_copy(lax.rem(r + d, R), d).wait_recv(), 1)
    for m in range(R // per):
        group = [fin[per * m + i].astype(F32) for i in range(per)]
        block = jnp.concatenate([g[:hs] for g in group], axis=0)
        gw_o[:, pl.ds(m * tile, tile)] = jnp.transpose(block, (1, 0))
        gb_o[:, pl.ds(m * tile, tile)] = sum(g[hs:hs + 1] for g in group)

    each(R // 2, lambda d: t_direct(d).wait_send(), 1)
    each(R // 2, lambda d: t_forward(d).wait_send())
    each(L // 2, lambda d: p_direct(L // 2 - d).wait_send(), 1)
    each(L // 2, lambda d: p_forward(d).wait_send())
    each(L, lambda d: q_copy(d).wait_send(), 1)
    each(L, lambda d: w_copy(d).wait_send(), 1)

    def rep_sent(d):
        rep_copy(act_all, mine, a_send.at[d], a_recv.at[r], d).wait_send()
        rep_copy(gp_all, mine, g_send.at[d], g_recv.at[r], d).wait_send()
        f_copy(r, d).wait_send()

    each(R, rep_sent, 1)


def write_kernel(*refs):
    n = (len(refs) - 1) // 2
    copies = [pltpu.make_async_copy(refs[i], refs[n + i], refs[-1].at[i]) for i in range(n)]
    for copy in copies:
        copy.start()
    for copy in copies:
        copy.wait()


def write_out(*arrays):
    n = len(arrays)
    return pl.pallas_call(
        write_kernel,
        out_shape=tuple(jax.ShapeDtypeStruct(a.shape, a.dtype) for a in arrays),
        in_specs=[pl.BlockSpec(memory_space=pltpu.VMEM)] * n,
        out_specs=(pl.BlockSpec(memory_space=pltpu.HBM),) * n,
        scratch_shapes=[pltpu.SemaphoreType.DMA((n,))],
        name="write_out",
    )(*[pltpu.with_memory_space_constraint(a, pltpu.VMEM) for a in arrays])


def local(features, weight, out_bias, tile_values, tile_rows, tile_cols, tile_counts, cotangent):
    L, R = lax.axis_size("layer"), lax.axis_size("rep")
    rows_dev, hidden = cotangent.shape
    f_in = features.shape[1]
    tile = tile_values.shape[-1]
    slots = tile_values.shape[2]
    nt = rows_dev // tile
    hs = hidden // R
    metas = slots * 2 * nt
    vmem = pl.BlockSpec(memory_space=pltpu.VMEM)
    hbm = pl.BlockSpec(memory_space=pltpu.HBM)
    sem = pltpu.SemaphoreType.DMA
    grad_scale = 1.0 / math.sqrt(rows_dev * L)
    act, gf, gw, gb = pl.pallas_call(
        functools.partial(kernel, L, R, grad_scale),
        out_shape=(
            jax.ShapeDtypeStruct((rows_dev, hidden), BF),
            jax.ShapeDtypeStruct((rows_dev, f_in), BF),
            jax.ShapeDtypeStruct((f_in, hidden), F32),
            jax.ShapeDtypeStruct((1, hidden), F32),
        ),
        in_specs=[hbm] * 8,
        out_specs=(vmem, vmem, vmem, vmem),
        scratch_shapes=[
            pltpu.VMEM(features.shape, BF),
            pltpu.VMEM(weight.shape, BF),
            pltpu.VMEM((1, hidden), F32),
            pltpu.VMEM(tile_values.shape, BF),
            pltpu.SMEM(tile_rows.shape, jnp.int32),
            pltpu.SMEM(tile_rows.shape, jnp.int32),
            pltpu.SMEM(tile_rows.shape, jnp.int32),
            pltpu.VMEM(cotangent.shape, BF),
            sem((8,)),
            pltpu.VMEM((L, slots * tile + metas, tile), BF),
            pltpu.VMEM((hidden, f_in), BF),
            pltpu.VMEM((hidden, tile), F32),
            pltpu.VMEM((nt, hidden, tile), BF),
            pltpu.VMEM((L, nt, hs, tile), BF),
            pltpu.VMEM((nt, hs, tile), F32),
            pltpu.VMEM((nt, hs, tile), BF),
            pltpu.VMEM((nt, hidden, tile), BF),
            pltpu.VMEM((nt, hidden, tile), BF),
            pltpu.VMEM((L, slots * hs + metas, tile), BF),
            pltpu.VMEM((L, slots * hs + metas, tile), BF),
            pltpu.VMEM((L, hs + metas, tile), BF),
            pltpu.VMEM((R, hs + metas, tile), BF),
            sem((R,)), sem((R,)), sem((R,)),
            sem((L,)), sem((L,)), sem((L,)),
            sem((L,)), sem((L,)),
            sem((R,)), sem((R,)),
            sem((R,)), sem((R,)),
            sem((L,)), sem((L,)),
            sem((R,)), sem((R,)),
        ],
        compiler_params=pltpu.CompilerParams(
            collective_id=0, has_side_effects=True, vmem_limit_bytes=32 * 1024 * 1024
        ),
        name="graph_layer",
    )(*[pltpu.with_memory_space_constraint(x, pltpu.HBM) for x in (
        features, weight, out_bias.reshape(1, hidden), tile_values, tile_rows, tile_cols,
        tile_counts, cotangent)])
    return write_out(act, gf, gw, gb.reshape(hidden))


def solution(mesh):
    in_specs = (
        P("layer", None),
        P(),
        P(),
        P("layer", "rep", None, None, None),
        P("layer", "rep", None),
        P("layer", "rep", None),
        P("layer", "rep", None),
        P("layer", None),
    )
    out_specs = (P("layer", None), P("layer", None), P(), P())
    return jax.shard_map(local, mesh=mesh, in_specs=in_specs, out_specs=out_specs, check_vma=False)
```

```python
import functools
import math

import jax
import jax.numpy as jnp
from jax import lax
from jax.experimental import pallas as pl
from jax.experimental.pallas import tpu as pltpu
from jax.sharding import PartitionSpec as P

BF = jnp.bfloat16
F32 = jnp.float32
NT = (((1,), (1,)), ((), ()))
NN = (((1,), (0,)), ((), ()))
MESH = pl.DeviceIdType.MESH


def dot(a, b, dims):
    return lax.dot_general(a, b, dims, preferred_element_type=F32)


def kernel(
    L, R, grad_scale,
    feat_h, w_h, bias_h, tv_h, rows_h, cols_h, counts_h, cot_h,
    act_o, gf_o, gw_o, gb_o,
    feat, w, bias, tv, rows, cols, counts, cot, in_sem,
    tiles, wt, biasb, cot_t, proj, agg, grad, act_all, gp_all, psend, precv, gwbuf, fin,
    t_send, t_fwd, t_recv, p_send, p_fwd, p_recv, q_send, q_recv,
    a_send, a_recv, g_send, g_recv, w_send, w_recv, f_send, f_recv,
):
    l = lax.axis_index("layer")
    r = lax.axis_index("rep")
    sections, slots, tile = tv.shape[1], tv.shape[2], tv.shape[3]
    hidden = w.shape[1]
    hs = hidden // R
    nt = feat.shape[0] // tile
    meta_at = slots * tile
    metas = tiles.shape[1] - meta_at
    mine = pl.ds(pl.multiple_of(r * hs, hs), hs)

    def remote(src, dst, ssem, rsem, pl_, pr_):
        return pltpu.make_async_remote_copy(
            src_ref=src, dst_ref=dst, send_sem=ssem, recv_sem=rsem,
            device_id={"layer": pl_, "rep": pr_}, device_id_type=MESH,
        )

    def each(n, fn, start=0):
        lax.fori_loop(start, n, lambda i, c: (fn(i), c)[1], 0)

    barrier = pltpu.get_barrier_semaphore()
    loads = [
        pltpu.make_async_copy(src, dst, in_sem.at[i])
        for i, (src, dst) in enumerate((
            (counts_h, counts), (rows_h, rows), (cols_h, cols), (tv_h, tv),
            (w_h, w), (feat_h, feat), (bias_h, bias), (cot_h, cot)))
    ]
    for load in loads:
        load.start()

    def greet_layer(d):
        pl.semaphore_signal(
            barrier, inc=1, device_id={"layer": lax.rem(l + d, L), "rep": r}, device_id_type=MESH)

    def greet_rep(d):
        pl.semaphore_signal(
            barrier, inc=1, device_id={"layer": l, "rep": lax.rem(r + d, R)}, device_id_type=MESH)

    each(L, greet_layer, 1)
    each(R, greet_rep, 1)

    for load in loads[:4]:
        load.wait()
    lanes = lax.broadcasted_iota(jnp.int32, (tile, tile), 1)
    row_ids = lax.broadcasted_iota(jnp.int32, (metas, tile), 0)
    for j in range(sections):
        meta = jnp.zeros((metas, tile), F32)
        at = r * sections + j
        for k in range(slots):
            live = jnp.where(lanes < counts[0, j, k], tv[0, j, k].astype(F32), 0.0)
            tiles[at, pl.ds(k * tile, tile), :] = live.astype(BF)
            base = 2 * nt * k
            meta = meta + jnp.where(row_ids == base + rows[0, j, k], 1.0, 0.0)
            meta = meta + jnp.where(row_ids == base + nt + cols[0, j, k], 1.0, 0.0)
        tiles[at, pl.ds(meta_at, metas), :] = meta.astype(BF)

    for load in loads[4:6]:
        load.wait()
    wt[...] = jnp.transpose(w[...].astype(F32), (1, 0)).astype(BF)
    own = dot(wt[mine, :], feat[...], NT).astype(BF)
    for t in range(nt):
        proj[l, t] = own[:, t * tile:(t + 1) * tile]

    pl.semaphore_wait(barrier, L - 1 + R - 1)

    twin_l = l + 1 - 2 * lax.rem(l, 2)
    twin_r = r + 1 - 2 * lax.rem(r, 2)

    def p_direct(d):
        p = lax.rem(l + 2 * d, L)
        return remote(proj.at[l], proj.at[l], p_send.at[d], p_recv.at[l], p, r)

    def p_forward(d):
        p = lax.rem(l + 2 * d, L)
        return remote(proj.at[p], proj.at[p], p_fwd.at[d], p_recv.at[p], twin_l, r)

    def p_arrival(p):
        return remote(proj.at[p], proj.at[p], p_fwd.at[0], p_recv.at[p], twin_l, r)

    def t_block(q):
        return tiles.at[pl.ds(q * sections, sections)]

    def t_direct(d):
        return remote(t_block(r), t_block(r), t_send.at[d], t_recv.at[r], l, lax.rem(r + 2 * d, R))

    def t_forward(d):
        q = lax.rem(r + 2 * d, R)
        return remote(t_block(q), t_block(q), t_fwd.at[d], t_recv.at[q], l, twin_r)

    def t_arrival(q):
        return remote(t_block(q), t_block(q), t_fwd.at[0], t_recv.at[q], l, twin_r)

    each(R // 2, lambda d: t_direct(d).start(), 1)
    each(L // 2, lambda d: p_direct(L // 2 - d).start(), 1)
    p_forward(0).start()
    t_forward(0).start()

    for load in loads[6:]:
        load.wait()
    biasb[...] = jnp.transpose(jnp.broadcast_to(bias[...], (tile, hidden)), (1, 0))
    for t in range(nt):
        part = cot[pl.ds(t * tile, tile), :].astype(F32)
        cot_t[t] = jnp.transpose(part, (1, 0)).astype(BF)

    def relay_tiles(d):
        t_arrival(lax.rem(r + 2 * d, R)).wait_recv()
        t_forward(d).start()

    def relay_proj(d):
        p_arrival(lax.rem(l + 2 * d, L)).wait_recv()
        p_forward(d).start()

    each(R // 2, relay_tiles, 1)
    each(L // 2, relay_proj, 1)
    each(R // 2, lambda d: t_arrival(lax.rem(twin_r + 2 * d, R)).wait_recv())

    agg[...] = jnp.zeros_like(agg)

    def section(s):
        meta = tiles[s, pl.ds(meta_at, metas), :].astype(F32)
        blocks = [proj[s, c].astype(F32) for c in range(nt)]
        sums = [agg[t] for t in range(nt)]
        for k in range(slots):
            base = 2 * nt * k
            picked = sum(
                meta[base + nt + c:base + nt + c + 1, :] * blocks[c] for c in range(nt)
            ).astype(BF)
            product = dot(picked, tiles[s, pl.ds(k * tile, tile), :], NT)
            for t in range(nt):
                sums[t] = sums[t] + meta[base + t:base + t + 1, :] * product
        for t in range(nt):
            agg[t] = sums[t]

    each(L // 2, lambda d: section(lax.rem(l + 2 * d, L)))

    def late_section(d):
        p = lax.rem(twin_l + 2 * d, L)
        p_arrival(p).wait_recv()
        section(p)

    each(L // 2, late_section)

    own_bias = biasb[mine, :]
    for t in range(nt):
        pre = proj[l, t].astype(F32) + agg[t] + own_bias
        sig = jax.nn.sigmoid(pre)
        act_all[t, mine, :] = (pre * sig).astype(BF)
        grad[t] = (cot_t[t, mine, :].astype(F32) * sig * (1.0 + pre * (1.0 - sig))).astype(BF)

    def rep_copy(buf, at, ssem, rsem, d):
        return remote(buf.at[:, at, :], buf.at[:, at, :], ssem, rsem, l, lax.rem(r + d, R))

    def q_copy(d):
        s = lax.rem(l + d, L)
        return remote(psend.at[s], precv.at[l], q_send.at[d], q_recv.at[l], s, r)

    def products(s, out, at):
        raw = tiles[s, pl.ds(meta_at, metas), :]
        meta = raw.astype(F32)
        blocks = [grad[t].astype(F32) for t in range(nt)]
        for k in range(slots):
            base = 2 * nt * k
            picked = sum(
                meta[base + t:base + t + 1, :] * blocks[t] for t in range(nt)
            ).astype(BF)
            out[at, pl.ds(k * hs, hs), :] = dot(
                picked, tiles[s, pl.ds(k * tile, tile), :], NN).astype(BF)
        out[at, pl.ds(slots * hs, metas), :] = raw

    def send_products(d):
        s = lax.rem(l + d, L)
        products(s, psend, s)
        q_copy(d).start()

    each(L // 2, lambda d: send_products(L - d), 1)
    each(R, lambda d: rep_copy(act_all, mine, a_send.at[d], a_recv.at[r], d).start(), 1)
    each(L, lambda d: send_products(L - d), L // 2)

    def rep_slice(q):
        return pl.ds(pl.multiple_of(q * hs, hs), hs)

    products(l, precv, l)

    def a_wait(d):
        q = lax.rem(r + d, R)
        rep_copy(act_all, rep_slice(q), a_send.at[d], a_recv.at[q], d).wait_recv()

    each(R, a_wait, 1)
    for t in range(nt):
        act_o[pl.ds(t * tile, tile), :] = jnp.transpose(
            act_all[t].astype(F32), (1, 0)).astype(BF)

    for t in range(nt):
        agg[t] = grad[t].astype(F32)

    def add_products(p):
        meta = precv[p, pl.ds(slots * hs, metas), :].astype(F32)
        for c in range(nt):
            total = agg[c]
            for k in range(slots):
                at = 2 * nt * k + nt + c
                total = total + meta[at:at + 1, :] * precv[p, pl.ds(k * hs, hs), :].astype(F32)
            agg[c] = total

    gb = jnp.zeros((metas, tile), F32)
    per = tile // hs
    ones = jnp.ones((metas, tile), BF)
    for t in range(nt):
        gb = gb + dot(ones, jnp.concatenate([grad[t]] * per, axis=0), NT)
    half = lax.broadcasted_iota(jnp.int32, (metas, tile), 1) // hs
    gwbuf[l, pl.ds(hs, metas), :] = jnp.where(half == lax.rem(r, per), gb, 0.0).astype(BF)

    add_products(l)

    def take_products(d):
        p = lax.rem(l + d, L)
        remote(precv.at[p], precv.at[p], q_send.at[d], q_recv.at[p], p, r).wait_recv()
        add_products(p)

    each(L, take_products, 1)

    for t in range(nt):
        gp_all[t, mine, :] = agg[t].astype(BF)
    each(R, lambda d: rep_copy(gp_all, mine, g_send.at[d], g_recv.at[r], d).start(), 1)

    gw = dot(jnp.concatenate([agg[t].astype(BF) for t in range(nt)], axis=1), feat[...], NN)
    gwbuf[l, pl.ds(0, hs), :] = gw.astype(BF)

    def w_copy(d):
        return remote(gwbuf.at[l], gwbuf.at[l], w_send.at[d], w_recv.at[l], lax.rem(l + d, L), r)

    each(L, lambda d: w_copy(d).start(), 1)

    def g_wait(d):
        q = lax.rem(r + d, R)
        rep_copy(gp_all, rep_slice(q), g_send.at[d], g_recv.at[q], d).wait_recv()

    def w_wait(d):
        p = lax.rem(l + d, L)
        remote(gwbuf.at[p], gwbuf.at[p], w_send.at[d], w_recv.at[p], p, r).wait_recv()

    each(L, w_wait, 1)
    fin[r] = (
        lax.fori_loop(0, L, lambda p, c: c + gwbuf[p].astype(F32),
                      jnp.zeros((hs + metas, tile), F32)) * grad_scale
    ).astype(BF)

    def f_copy(q, d):
        return remote(fin.at[q], fin.at[q], f_send.at[d], f_recv.at[q], l, lax.rem(r + d, R))

    each(R, lambda d: f_copy(r, d).start(), 1)

    each(R, g_wait, 1)
    for t in range(nt):
        turned = jnp.transpose(gp_all[t].astype(F32), (1, 0)).astype(BF)
        gf_o[pl.ds(t * tile, tile), :] = dot(turned, w[...], NT).astype(BF)

    each(R, lambda d: f_copy(lax.rem(r + d, R), d).wait_recv(), 1)
    for m in range(R // per):
        group = [fin[per * m + i].astype(F32) for i in range(per)]
        block = jnp.concatenate([g[:hs] for g in group], axis=0)
        gw_o[:, pl.ds(m * tile, tile)] = jnp.transpose(block, (1, 0))
        gb_o[:, pl.ds(m * tile, tile)] = sum(g[hs:hs + 1] for g in group)

    each(R // 2, lambda d: t_direct(d).wait_send(), 1)
    each(R // 2, lambda d: t_forward(d).wait_send())
    each(L // 2, lambda d: p_direct(L // 2 - d).wait_send(), 1)
    each(L // 2, lambda d: p_forward(d).wait_send())
    each(L, lambda d: q_copy(d).wait_send(), 1)
    each(L, lambda d: w_copy(d).wait_send(), 1)

    def rep_sent(d):
        rep_copy(act_all, mine, a_send.at[d], a_recv.at[r], d).wait_send()
        rep_copy(gp_all, mine, g_send.at[d], g_recv.at[r], d).wait_send()
        f_copy(r, d).wait_send()

    each(R, rep_sent, 1)


def write_kernel(*refs):
    n = (len(refs) - 1) // 2
    copies = [pltpu.make_async_copy(refs[i], refs[n + i], refs[-1].at[i]) for i in range(n)]
    for copy in copies:
        copy.start()
    for copy in copies:
        copy.wait()


def write_out(*arrays):
    n = len(arrays)
    return pl.pallas_call(
        write_kernel,
        out_shape=tuple(jax.ShapeDtypeStruct(a.shape, a.dtype) for a in arrays),
        in_specs=[pl.BlockSpec(memory_space=pltpu.VMEM)] * n,
        out_specs=(pl.BlockSpec(memory_space=pltpu.HBM),) * n,
        scratch_shapes=[pltpu.SemaphoreType.DMA((n,))],
        name="write_out",
    )(*[pltpu.with_memory_space_constraint(a, pltpu.VMEM) for a in arrays])


def local(features, weight, out_bias, tile_values, tile_rows, tile_cols, tile_counts, cotangent):
    L, R = lax.axis_size("layer"), lax.axis_size("rep")
    rows_dev, hidden = cotangent.shape
    f_in = features.shape[1]
    tile = tile_values.shape[-1]
    slots = tile_values.shape[2]
    nt = rows_dev // tile
    hs = hidden // R
    metas = slots * 2 * nt
    vmem = pl.BlockSpec(memory_space=pltpu.VMEM)
    hbm = pl.BlockSpec(memory_space=pltpu.HBM)
    sem = pltpu.SemaphoreType.DMA
    grad_scale = 1.0 / math.sqrt(rows_dev * L)
    act, gf, gw, gb = pl.pallas_call(
        functools.partial(kernel, L, R, grad_scale),
        out_shape=(
            jax.ShapeDtypeStruct((rows_dev, hidden), BF),
            jax.ShapeDtypeStruct((rows_dev, f_in), BF),
            jax.ShapeDtypeStruct((f_in, hidden), F32),
            jax.ShapeDtypeStruct((1, hidden), F32),
        ),
        in_specs=[hbm] * 8,
        out_specs=(vmem, vmem, vmem, vmem),
        scratch_shapes=[
            pltpu.VMEM(features.shape, BF),
            pltpu.VMEM(weight.shape, BF),
            pltpu.VMEM((1, hidden), F32),
            pltpu.VMEM(tile_values.shape, BF),
            pltpu.SMEM(tile_rows.shape, jnp.int32),
            pltpu.SMEM(tile_rows.shape, jnp.int32),
            pltpu.SMEM(tile_rows.shape, jnp.int32),
            pltpu.VMEM(cotangent.shape, BF),
            sem((8,)),
            pltpu.VMEM((L, slots * tile + metas, tile), BF),
            pltpu.VMEM((hidden, f_in), BF),
            pltpu.VMEM((hidden, tile), F32),
            pltpu.VMEM((nt, hidden, tile), BF),
            pltpu.VMEM((L, nt, hs, tile), BF),
            pltpu.VMEM((nt, hs, tile), F32),
            pltpu.VMEM((nt, hs, tile), BF),
            pltpu.VMEM((nt, hidden, tile), BF),
            pltpu.VMEM((nt, hidden, tile), BF),
            pltpu.VMEM((L, slots * hs + metas, tile), BF),
            pltpu.VMEM((L, slots * hs + metas, tile), BF),
            pltpu.VMEM((L, hs + metas, tile), BF),
            pltpu.VMEM((R, hs + metas, tile), BF),
            sem((R,)), sem((R,)), sem((R,)),
            sem((L,)), sem((L,)), sem((L,)),
            sem((L,)), sem((L,)),
            sem((R,)), sem((R,)),
            sem((R,)), sem((R,)),
            sem((L,)), sem((L,)),
            sem((R,)), sem((R,)),
        ],
        compiler_params=pltpu.CompilerParams(
            collective_id=0, has_side_effects=True, vmem_limit_bytes=32 * 1024 * 1024
        ),
        name="graph_layer",
    )(*[pltpu.with_memory_space_constraint(x, pltpu.HBM) for x in (
        features, weight, out_bias.reshape(1, hidden), tile_values, tile_rows, tile_cols,
        tile_counts, cotangent)])
    return write_out(act, gf, gw, gb.reshape(hidden))


def solution(mesh):
    in_specs = (
        P("layer", None),
        P(),
        P(),
        P("layer", "rep", None, None, None),
        P("layer", "rep", None),
        P("layer", "rep", None),
        P("layer", "rep", None),
        P("layer", None),
    )
    out_specs = (P("layer", None), P("layer", None), P(), P())
    return jax.shard_map(local, mesh=mesh, in_specs=in_specs, out_specs=out_specs, check_vma=False)
```
